32 devices in a mesh: tm: 8 (over z, x), col: 4 (over y, core).
Axes of the slice: x: 2, y: 2, z: 4, core: 2. Of those that a mesh axis runs over, the one named last changes fastest.
Arguments:
- jacobians: float32 [96, 512, 512], P('tm'), may hold values from -0.05 to 1.05
- increments: float32 [96, 512], P('tm'), may hold values from -1.5 to 1.5
- initial: float32 [512], P('col'), may hold values from -6 to 6
Outputs:
- states: float32 [96, 512], P('tm', 'col')
The draws below stay inside these ranges and needn't reach their ends.
All inputs are finite; a program needn't handle non-finite values.
Results may differ from the reference program's by a relative error of at most 0.0003.
Values sent between devices are 32-bit elements; how exact they have to be, the bound alone decides.
No kernel may reach another device: no remote copies, remote signals or barrier semaphores. Data moves between devices by JAX's collectives and lax.ppermute only.
A program may use at most 128 MiB of HBM per device.

```python
import jax
import jax.numpy as jnp
from jax import lax

NB = 512
STEP_DEV = 12
HORIZON_STEPS = 96


def draw_jacobians(key, part):
    random_key_list = jax.random.split(key, 6)
    slow_share = 0.5
    is_slow = jax.random.uniform(random_key_list[0], (NB,)) < slow_share
    spread = jax.random.uniform(random_key_list[1], (NB,))
    lower_log = jnp.log(0.1 / HORIZON_STEPS)
    middle_log = jnp.log(0.6 / HORIZON_STEPS)
    upper_log = jnp.log(0.125)
    slow_rate = jnp.exp(lower_log + spread * (middle_log - lower_log))
    fast_rate = jnp.exp(middle_log + spread * (upper_log - middle_log))
    link_rate = jnp.where(is_slow, slow_rate, fast_rate)
    segment_of = jnp.arange(HORIZON_STEPS) // STEP_DEV
    segment_factor = jnp.exp(jax.random.uniform(random_key_list[2], (HORIZON_STEPS // STEP_DEV,), minval=-0.7, maxval=0.7))[segment_of]
    step_factor = jax.random.uniform(random_key_list[3], (HORIZON_STEPS,), minval=0.6, maxval=1.4)
    surge_factor = jnp.where(jax.random.uniform(random_key_list[4], (HORIZON_STEPS,)) < 3.0 / HORIZON_STEPS, 0.7, 1.0)
    diagonal_entries = jnp.exp(-link_rate[None, :] * (segment_factor * step_factor)[:, None]) * surge_factor[:, None]
    coupling = 0.04 * jnp.clip(jax.random.normal(random_key_list[5], (HORIZON_STEPS, NB, NB)), -6.0, 6.0) / jnp.sqrt(float(NB))
    return (coupling + diagonal_entries[:, :, None] * jnp.eye(NB, dtype=jnp.float32)[None]).astype(jnp.float32)


def levels(own_key, dims, cuts, smallest, largest):
    level, own = 1.0, jax.random.fold_in(own_key, 6)
    for axis_at, parts in cuts:
        draws = jnp.exp(jax.random.uniform(jax.random.fold_in(own, axis_at), (parts,), jnp.float32, smallest / len(cuts), largest / len(cuts)))
        level = level * jnp.repeat(draws, dims[axis_at] // parts).reshape([-1 if axis == axis_at else 1 for axis in range(len(dims))])
    return level


def gaussian(stream_key, shape, scale, reach, pieces=(), kind=jnp.bfloat16):
    gain = levels(stream_key, shape, pieces, -0.22, 0.18) if pieces else 1.0
    entries = jax.random.normal(stream_key, shape, jnp.float32) * scale * gain
    return jnp.minimum(jnp.maximum(entries, -reach), reach).astype(kind)


def setup_inputs(seed: int = 0) -> dict:
    seeds = jax.random.split(jax.random.key(seed), 4)
    jacobians = draw_jacobians(jax.random.fold_in(seeds[3], 71), 0)
    increments = gaussian(seeds[1], (HORIZON_STEPS, NB), 0.1, 1.5, ((0, 8),), jnp.float32)
    initial = gaussian(seeds[2], (NB,), 1.0, 6.0, ((0, 4),), jnp.float32)
    return dict(jacobians=jacobians, increments=increments, initial=initial)


def reference(jacobians, increments, initial):
    def advance(current, inputs):
        step_jac, step_inc = inputs
        following = jnp.dot(step_jac, current, precision=lax.Precision.HIGHEST, preferred_element_type=jnp.float32) + step_inc
        return following, following

    _, states = lax.scan(advance, initial.astype(jnp.float32), (jacobians, increments))
    return states
```

```python
import functools

import jax
import jax.numpy as jnp
from jax import lax
from jax.experimental import pallas as pl
from jax.experimental.pallas import tpu as pltpu
from jax.sharding import PartitionSpec as P

AXES = ("tm", "col")
LANES = 128
DIRECT = 3
VMEM = pl.BlockSpec(memory_space=pltpu.VMEM)


def swap_pairs(size, moved):
    target = dict(moved)
    for device in range(size):
        partner = device ^ 1
        if device not in target and partner < size and partner not in target:
            target[device] = partner
            target[partner] = device
    return sorted(target.items())


def hop(block, segment):
    segments, parts = lax.axis_size("tm"), lax.axis_size("col")
    moved = {}
    for part in range(parts):
        here = segment * parts + part
        there = here + parts
        moved[here] = there
        moved[there] = here
    return lax.ppermute(block, AXES, swap_pairs(segments * parts, moved))


def gather_parts(own):
    parts = lax.axis_size("col")
    index = lax.axis_index("col")
    width = own.shape[1]
    full = lax.dynamic_update_slice(
        jnp.zeros((1, width * parts), own.dtype), own, (jnp.int32(0), index * width)
    )
    bit = 1
    while bit < parts:
        route = [(i, i ^ bit) for i in range(parts)]
        full = full + lax.ppermute(full, "col", route)
        bit *= 2
    return full


def apply_map(rows_of, offset, vector):
    order = vector.shape[1]
    diagonal = lax.broadcasted_iota(jnp.int32, (LANES, LANES), 0) == lax.broadcasted_iota(
        jnp.int32, (LANES, LANES), 1
    )
    pieces = []
    for top in range(0, order, LANES):
        total = None
        for left in range(0, order, LANES):
            term = rows_of(top, left) * vector[:, left : left + LANES]
            total = term if total is None else total + term
        column = jnp.sum(total, axis=1, keepdims=True)
        pieces.append(jnp.sum(jnp.where(diagonal, column, 0.0), axis=0, keepdims=True))
    return jnp.concatenate(pieces, axis=1) + offset


def step(jac, inc, t, vector):
    return apply_map(
        lambda top, left: jac[t, pl.ds(top, LANES), pl.ds(left, LANES)],
        inc[pl.ds(t, 1), :],
        vector,
    )


def run_segment(jac, inc, vector):
    return lax.fori_loop(0, jac.shape[0], lambda t, v: step(jac, inc, t, v), vector)


def halves(value):
    high = value.astype(jnp.bfloat16)
    return high, (value - high.astype(jnp.float32)).astype(jnp.bfloat16)


def product(left, right):
    left_high, left_low = halves(left)
    right_high, right_low = halves(right)

    def dot(a, b):
        return jnp.dot(a, b, preferred_element_type=jnp.float32)

    return dot(left_high, right_high) + (dot(left_high, right_low) + dot(left_low, right_high))


def compose_kernel(jac, inc, start, out, whole, offset):
    segment = lax.axis_index("tm")
    steps = jac.shape[0]

    @pl.when(segment == 0)
    def _():
        out[...] = run_segment(jac, inc, start[...])

    @pl.when(segment >= DIRECT)
    def _():
        offset[...] = run_segment(jac, inc, jnp.zeros_like(start))
        whole[...] = jac[0]

        def body(t, carry):
            whole[...] = product(jac[t], whole[...])
            return carry

        lax.fori_loop(1, steps, body, 0)


def hop_kernel(k, jac, inc, whole, offset, received, kept, out, start):
    here = lax.axis_index("tm") == k

    @pl.when(here)
    def _():
        vector = received[...]
        start[...] = vector
        if k < DIRECT:
            out[...] = run_segment(jac, inc, vector)
        else:
            out[...] = apply_map(
                lambda top, left: whole[pl.ds(top, LANES), pl.ds(left, LANES)],
                offset[...],
                vector,
            )

    @pl.when(jnp.logical_not(here))
    def _():
        start[...] = kept[...]
        out[...] = kept[...]


def states_kernel(last, jac, inc, received, kept, out):
    index = lax.axis_index("tm")
    part = out.shape[1]
    first = pl.multiple_of(lax.axis_index("col") * part, part)
    vector = jnp.where(index == last, received[...], kept[...])

    def body(t, v):
        v = step(jac, inc, t, v)
        hidden = lax.broadcasted_iota(jnp.int32, v.shape, 1)
        own = v[:, 0:part]
        for other in range(1, v.shape[1] // part):
            own = jnp.where(first == other * part, v[:, other * part : (other + 1) * part], own)
        out[pl.ds(t, 1), :] = own
        return v

    lax.fori_loop(0, jac.shape[0], body, vector)


def call(kernel, outs, *args, limit=8 << 20):
    return pl.pallas_call(
        kernel,
        out_shape=outs,
        in_specs=[VMEM] * len(args),
        out_specs=jax.tree.map(lambda _: VMEM, outs),
        compiler_params=pltpu.CompilerParams(vmem_limit_bytes=limit),
    )(*args)


def body(jacobians, increments, initial):
    segments = lax.axis_size("tm")
    steps, order, _ = jacobians.shape
    jac = pltpu.with_memory_space_constraint(jacobians, pltpu.VMEM)
    row = pltpu.VMEM((1, order), jnp.float32)
    start0 = gather_parts(initial[None, :])
    out, whole, offset = call(
        compose_kernel,
        (row, pltpu.VMEM((order, order), jnp.float32), row),
        jac,
        increments,
        start0,
        limit=24 << 20,
    )
    kept = start0
    for k in range(1, segments):
        received = hop(out, k - 1)
        if k == segments - 1:
            break
        out, kept = call(
            functools.partial(hop_kernel, k), (row, row), jac, increments, whole, offset, received, kept
        )
    return call(
        functools.partial(states_kernel, segments - 1),
        jax.ShapeDtypeStruct((steps, initial.shape[0]), jnp.float32),
        jac,
        increments,
        received,
        kept,
    )


def solution(mesh):
    return jax.shard_map(
        body,
        mesh=mesh,
        in_specs=(P("tm", None, None), P("tm", None), P("col")),
        out_specs=P("tm", "col"),
        check_vma=False,
    )
```

```python
import functools

import jax
import jax.numpy as jnp
from jax import lax
from jax.experimental import pallas as pl
from jax.experimental.pallas import tpu as pltpu
from jax.sharding import PartitionSpec as P

AXES = ("tm", "col")
LANES = 128
VMEM = pl.BlockSpec(memory_space=pltpu.VMEM)
FAR = pl.BlockSpec(memory_space=pltpu.HBM)


def factors(segment, steps):
    wanted = 3 * segment + 1
    if isinstance(segment, int):
        return min(steps - 1, wanted)
    return jnp.minimum(steps - 1, wanted)


def swap_routes(size, moved):
    target = dict(moved)
    for device in range(size):
        partner = device ^ 1
        if device not in target and partner < size and partner not in target:
            target[device] = partner
            target[partner] = device
    return sorted(target.items())


def hop(block, segment, twist=0, rejoin=0):
    segments, parts = lax.axis_size("tm"), lax.axis_size("col")
    moved = {}
    for part in range(parts):
        here = segment * parts + part
        there = (segment + 1) * parts + (part ^ twist)
        moved[here] = there
        moved[there] = here
        if rejoin:
            moved[part] = part ^ rejoin
    return lax.ppermute(block, AXES, swap_routes(segments * parts, moved))


def swap_parts(block):
    parts = lax.axis_size("col")
    return lax.ppermute(block, "col", [(i, i ^ 1) for i in range(parts)])


def reduce_rows(total):
    diagonal = lax.broadcasted_iota(jnp.int32, (LANES, LANES), 0) == lax.broadcasted_iota(
        jnp.int32, (LANES, LANES), 1
    )
    column = jnp.sum(total, axis=1, keepdims=True)
    return jnp.sum(jnp.where(diagonal, column, 0.0), axis=0, keepdims=True)


def apply_block(rows_of, vector):
    total = None
    for left in range(0, vector.shape[1], LANES):
        term = rows_of(left) * vector[:, left : left + LANES]
        total = term if total is None else total + term
    return reduce_rows(total)


def apply_map(block_of, offset, vector):
    pieces = [
        apply_block(functools.partial(block_of, top), vector)
        for top in range(0, vector.shape[1], LANES)
    ]
    return jnp.concatenate(pieces, axis=1) + offset


def apply_whole(whole, offset, vector):
    return apply_map(
        lambda top, left: whole[pl.ds(top, LANES), pl.ds(left, LANES)], offset, vector
    )


def step(jac, inc, t, vector):
    return apply_map(
        lambda top, left: jac[t, pl.ds(top, LANES), pl.ds(left, LANES)],
        inc[pl.ds(t, 1), :],
        vector,
    )


def run_steps(jac, inc, first, last, vector):
    return lax.fori_loop(first, last, lambda t, v: step(jac, inc, t, v), vector)


def own_part(vector, part):
    index = lax.axis_index("col")
    own = vector[:, 0:part]
    for other in range(1, vector.shape[1] // part):
        own = jnp.where(index == other, vector[:, other * part : (other + 1) * part], own)
    return own


def halves(value):
    high = value.astype(jnp.bfloat16)
    return high, (value - high.astype(jnp.float32)).astype(jnp.bfloat16)


def product(left, right):
    left_high, left_low = halves(left)
    right_high, right_low = halves(right)

    def dot(a, b):
        return jnp.dot(a, b, preferred_element_type=jnp.float32)

    return dot(left_high, right_high) + (dot(left_high, right_low) + dot(left_low, right_high))


def first_kernel(jac_far, inc_far, own_far, jac, inc, sent, whole, offset, rows, offs, own, sems):
    steps, order, _ = jac.shape
    width = own.shape[1]
    segment = lax.axis_index("tm")
    index = lax.axis_index("col")

    def jac_copy(t):
        return pltpu.make_async_copy(jac_far.at[t], jac.at[t], sems.at[t])

    small = [
        pltpu.make_async_copy(own_far, own, sems.at[steps]),
        pltpu.make_async_copy(inc_far, inc, sems.at[steps + 1]),
    ]
    for copy in small:
        copy.start()
    for t in range(steps):
        jac_copy(t).start()
    for copy in small:
        copy.wait()

    @pl.when(segment == 0)
    def _():
        block = own[...]
        zero = jnp.zeros_like(block)
        vector = jnp.concatenate(
            [jnp.where(index == place, block, zero) for place in range(order // width)], axis=1
        )
        sent[:, order:] = vector

        def body(t, current):
            jac_copy(t).wait()
            added = inc[pl.ds(t, 1), :]
            return apply_map(
                lambda top, left: jac[t, pl.ds(top, LANES), pl.ds(left, LANES)],
                jnp.where(index == 0, added, jnp.zeros_like(added)),
                current,
            )

        sent[:, :order] = lax.fori_loop(0, steps, body, vector)

    @pl.when(segment > 0)
    def _():
        own_rows = pl.ds(pl.multiple_of(index * width, width), width)
        jac_copy(0).wait()
        whole[...] = jac[0]
        rows[0] = jac[0, own_rows, :]
        first = inc[0:1, :]
        offs[0:1, :] = own_part(first, width)
        count = factors(segment, steps)

        def body(t, carry):
            jac_copy(t).wait()
            whole[...] = product(jac[t], whole[...])
            carry = step(jac, inc, t, carry)
            rows[t] = whole[own_rows, :]
            offs[pl.ds(t, 1), :] = own_part(carry, width)
            return carry

        offset[...] = lax.fori_loop(1, 1 + count, body, first)

        def finish(t, carry):
            jac_copy(t).wait()
            return carry

        lax.fori_loop(1 + count, steps, finish, 0)


def join_kernel(mine, theirs, out, kept):
    order = out.shape[1]
    total = mine[...] + theirs[...]
    out[...] = total[:, :order]
    kept[...] = total[:, order:]


def hop_kernel(k, rejoin, jac, inc, whole, offset, kept, *refs):
    received, (out, start) = refs[:-2], refs[-2:]
    here = lax.axis_index("tm") == k
    steps = jac.shape[0]

    @pl.when(here)
    def _():
        vector = received[0][...]
        for other in received[1:]:
            vector = vector + other[...]
        start[...] = vector
        done = 1 + factors(k, steps)
        vector = apply_whole(whole, offset[...], vector)
        out[...] = run_steps(jac, inc, done, steps, vector) if done < steps else vector

    @pl.when(jnp.logical_not(here))
    def _():
        vector = kept[...]
        if rejoin:
            vector = jnp.where(lax.axis_index("tm") == 0, vector + received[0][...], vector)
        start[...] = vector
        out[...] = vector


def write_states(segment, jac, inc, rows, offs, vector, out):
    steps, part = out.shape
    prepared = jnp.logical_and(segment > 0, factors(segment, steps) == steps - 1)

    @pl.when(prepared)
    def _():
        for t in range(steps):
            own = apply_block(lambda left, t=t: rows[t, :, pl.ds(left, LANES)], vector)
            out[pl.ds(t, 1), :] = own + offs[pl.ds(t, 1), :]

    @pl.when(jnp.logical_not(prepared))
    def _():
        def body(t, v):
            v = step(jac, inc, t, v)
            out[pl.ds(t, 1), :] = own_part(v, part)
            return v

        lax.fori_loop(0, steps, body, vector)


def states_kernel(last, jac, inc, rows, offs, kept, out):
    segment = lax.axis_index("tm")

    @pl.when(segment != last)
    def _():
        write_states(segment, jac, inc, rows, offs, kept[...], out)


def last_kernel(last, jac, inc, rows, offs, received, before, out, scratch, sem):
    del before
    segment = lax.axis_index("tm")

    @pl.when(segment == last)
    def _():
        write_states(segment, jac, inc, rows, offs, received[...], scratch)
        copy = pltpu.make_async_copy(scratch, out, sem)
        copy.start()
        copy.wait()


def call(kernel, outs, *args, limit=4 << 20, far=(), far_out=False, scratch=(), aliases=None, work=0):
    return pl.pallas_call(
        kernel,
        out_shape=outs,
        in_specs=[FAR if place in far else VMEM for place in range(len(args))],
        out_specs=jax.tree.map(lambda _: FAR if far_out else VMEM, outs),
        scratch_shapes=scratch,
        input_output_aliases=aliases or {},
        cost_estimate=pl.CostEstimate(flops=work, bytes_accessed=work, transcendentals=0),
        compiler_params=pltpu.CompilerParams(vmem_limit_bytes=limit),
    )(*args)


def body(jacobians, increments, initial):
    segments, parts = lax.axis_size("tm"), lax.axis_size("col")
    steps, order, _ = jacobians.shape
    width = initial.shape[0]
    f32 = jnp.float32
    row = pltpu.VMEM((1, order), f32)
    far = [
        pltpu.with_memory_space_constraint(array, pltpu.HBM)
        for array in (jacobians, increments, initial[None, :])
    ]
    jac, inc, sent, whole, offset, rows, offs = call(
        first_kernel,
        (
            pltpu.VMEM(jacobians.shape, f32),
            pltpu.VMEM(increments.shape, f32),
            pltpu.VMEM((1, 2 * order), f32),
            pltpu.VMEM((order, order), f32),
            row,
            pltpu.VMEM((steps, width, order), f32),
            pltpu.VMEM((steps, width), f32),
        ),
        *far,
        far=(0, 1, 2),
        limit=16 << 20,
        scratch=[pltpu.VMEM((1, width), f32), pltpu.SemaphoreType.DMA((steps + 2,))],
    )
    out, kept = call(join_kernel, (row, row), sent, swap_parts(sent))
    last = segments - 1
    for k in range(1, segments):
        if k == 1:
            received = [hop(out, 0, twist) for twist in range(0, parts, 2)]
        elif k == 3:
            received = [hop(out, 2, rejoin=2)]
        else:
            received = [hop(out, k - 1)]
        if k < last:
            out, kept = call(
                functools.partial(hop_kernel, k, k == 3),
                (row, row),
                jac,
                inc,
                whole,
                offset,
                kept,
                *received,
            )
    shape = jax.ShapeDtypeStruct((steps, width), f32)
    before = call(
        functools.partial(states_kernel, last),
        shape,
        jac,
        inc,
        rows,
        offs,
        kept,
        work=steps * order * order * 4,
    )
    return call(
        functools.partial(last_kernel, last),
        shape,
        jac,
        inc,
        rows,
        offs,
        received[0],
        before,
        far=(5,),
        far_out=True,
        scratch=[pltpu.VMEM((steps, width), f32), pltpu.SemaphoreType.DMA],
        aliases={5: 0},
    )


def solution(mesh):
    return jax.shard_map(
        body,
        mesh=mesh,
        in_specs=(P("tm", None, None), P("tm", None), P("col")),
        out_specs=P("tm", "col"),
        check_vma=False,
    )
```

```python
import functools

import jax
import jax.numpy as jnp
from jax import lax
from jax.experimental import pallas as pl
from jax.experimental.pallas import tpu as pltpu
from jax.sharding import PartitionSpec as P

AXES = ("tm", "col")
LANES = 128
MERGE = 3
JOINS = {2: (0,), 4: (1, 2, 3)}
VIAS = (-1, 0)
AHEAD = 7
STAGES = (6, 8, 10)
VMEM = pl.BlockSpec(memory_space=pltpu.VMEM)
FAR = pl.BlockSpec(memory_space=pltpu.HBM)


def smaller(a, b):
    return min(a, b) if isinstance(a, int) and isinstance(b, int) else jnp.minimum(a, b)


def first_factors(segment, steps):
    wanted = 3 * segment - 3 + (segment == 1)
    return smaller(smaller(wanted, AHEAD), steps - 1)


def factors(segment, steps):
    windows = segment - (segment == 1)
    return smaller(first_factors(segment, steps) + windows, steps - 1)


def swap_routes(size, moved):
    target = dict(moved)
    for device in range(size):
        partner = device ^ 1
        if device not in target and partner < size and partner not in target:
            target[device] = partner
            target[partner] = device
    return sorted(target.items())


def hop(block, segment, twist=0, via=None, joined=()):
    segments, parts = lax.axis_size("tm"), lax.axis_size("col")
    moved = {}
    for part in range(parts):
        here = segment * parts + part
        there = (segment + 1) * parts + (part ^ twist)
        moved[here] = there
        if via is None:
            moved[there] = here ^ 1 if segment + 2 == segments and parts % 2 == 0 else here
        else:
            moved[there] = via * parts + part
            moved[via * parts + part] = here
        for other in joined:
            moved[other * parts + part] = other * parts + (part ^ 2)
    return lax.ppermute(block, AXES, swap_routes(segments * parts, moved))


def swap_parts(block):
    parts = lax.axis_size("col")
    return lax.ppermute(block, "col", [(i, i ^ 1) for i in range(parts)])


def reduce_rows(total):
    diagonal = lax.broadcasted_iota(jnp.int32, (LANES, LANES), 0) == lax.broadcasted_iota(
        jnp.int32, (LANES, LANES), 1
    )
    column = jnp.sum(total, axis=1, keepdims=True)
    return jnp.sum(jnp.where(diagonal, column, 0.0), axis=0, keepdims=True)


def apply_block(rows_of, vector):
    total = None
    for left in range(0, vector.shape[1], LANES):
        term = rows_of(left) * vector[:, left : left + LANES]
        total = term if total is None else total + term
    return reduce_rows(total)


def apply_map(block_of, offset, vector):
    pieces = [
        apply_block(functools.partial(block_of, top), vector)
        for top in range(0, vector.shape[1], LANES)
    ]
    return jnp.concatenate(pieces, axis=1) + offset


def apply_whole(whole, offset, vector):
    return apply_map(
        lambda top, left: whole[pl.ds(top, LANES), pl.ds(left, LANES)], offset, vector
    )


def masked(keep, added):
    return added if keep is None else jnp.where(keep, added, jnp.zeros_like(added))


def step(jac, inc, t, vector, keep=None):
    return apply_map(
        lambda top, left: jac[t, pl.ds(top, LANES), pl.ds(left, LANES)],
        masked(keep, inc[pl.ds(t, 1), :]),
        vector,
    )


def run_steps(jac, inc, first, last, vector, keep):
    return lax.fori_loop(first, last, lambda t, v: step(jac, inc, t, v, keep), vector)


def own_part(vector, part):
    index = lax.axis_index("col")
    own = vector[:, 0:part]
    for other in range(1, vector.shape[1] // part):
        own = jnp.where(index == other, vector[:, other * part : (other + 1) * part], own)
    return own


def halves(value):
    high = value.astype(jnp.bfloat16)
    return high, (value - high.astype(jnp.float32)).astype(jnp.bfloat16)


def product(left, right):
    left_high, left_low = halves(left)
    right_high, right_low = halves(right)

    def dot(a, b):
        return jnp.dot(a, b, preferred_element_type=jnp.float32)

    return dot(left_high, right_high) + (dot(left_high, right_low) + dot(left_low, right_high))


def jac_copy(jac_far, jac, sems, t):
    return pltpu.make_async_copy(jac_far.at[t], jac.at[t], sems.at[t])


def stage_bounds(steps):
    return [0] + [min(stage, steps) for stage in STAGES] + [steps]


def add_factor(t, jac, inc, whole, rows, offs, carry):
    width = offs.shape[1]
    own_rows = pl.ds(pl.multiple_of(lax.axis_index("col") * width, width), width)
    whole[...] = product(jac[t], whole[...])
    carry = step(jac, inc, t, carry)
    rows[t] = whole[own_rows, :]
    offs[pl.ds(t, 1), :] = own_part(carry, width)
    return carry


def factor_kernel(window, jac_far, jac_in, inc, whole_in, offset_in, rows_in, offs_in, *refs):
    jac, whole, offset, rows, offs, sems = refs
    del jac_in, whole_in, offset_in, rows_in, offs_in
    steps = jac.shape[0]
    segment = lax.axis_index("tm")
    t = first_factors(segment, steps) + window + 1
    bounds = stage_bounds(steps)
    late = range(*bounds[window + 1 : window + 3]) if window < 2 else ()

    @pl.when(segment == 1)
    def _():
        for place in late:
            jac_copy(jac_far, jac, sems, place).start()

    @pl.when(jnp.logical_and(segment > max(window, 1), t < steps))
    def _():
        offset[...] = add_factor(t, jac, inc, whole, rows, offs, offset[...])

    @pl.when(segment == 1)
    def _():
        for place in late:
            jac_copy(jac_far, jac, sems, place).wait()


def first_kernel(jac_far, inc_far, own_far, jac, inc, sent, whole, offset, rows, offs, own, sems):
    steps, order, _ = jac.shape
    width = own.shape[1]
    segment = lax.axis_index("tm")
    index = lax.axis_index("col")
    soon = stage_bounds(steps)[1]
    now = jnp.where(segment == 1, soon, steps)

    def arrived(t):
        jac_copy(jac_far, jac, sems, t).wait()

    small = [
        pltpu.make_async_copy(own_far, own, sems.at[steps]),
        pltpu.make_async_copy(inc_far, inc, sems.at[steps + 1]),
    ]
    for copy in small:
        copy.start()
    for t in range(soon):
        jac_copy(jac_far, jac, sems, t).start()

    @pl.when(segment != 1)
    def _():
        for t in range(soon, steps):
            jac_copy(jac_far, jac, sems, t).start()

    for copy in small:
        copy.wait()

    @pl.when(segment == 0)
    def _():
        block = own[...]
        zero = jnp.zeros_like(block)
        vector = jnp.concatenate(
            [jnp.where(index == place, block, zero) for place in range(order // width)], axis=1
        )
        sent[:, order:] = vector

        def body(t, current):
            arrived(t)
            return step(jac, inc, t, current, index == 0)

        sent[:, :order] = lax.fori_loop(0, steps, body, vector)

    @pl.when(segment > 0)
    def _():
        own_rows = pl.ds(pl.multiple_of(index * width, width), width)
        arrived(0)
        whole[...] = jac[0]
        rows[0] = jac[0, own_rows, :]
        first = inc[0:1, :]
        offs[0:1, :] = own_part(first, width)
        count = first_factors(segment, steps)

        def body(t, carry):
            arrived(t)
            return add_factor(t, jac, inc, whole, rows, offs, carry)

        offset[...] = lax.fori_loop(1, 1 + count, body, first)

        def finish(t, carry):
            arrived(t)
            return carry

        lax.fori_loop(1 + count, now, finish, 0)


def join_kernel(mine, theirs, out, kept):
    order = out.shape[1]
    total = mine[...] + theirs[...]
    out[...] = total[:, :order]
    kept[...] = total[:, order:]


def hop_kernel(k, joined, far, inc, whole, offset, kept, *refs):
    jac = refs[0]
    if far:
        jac_far, received, (out, start, jac, sems) = refs[1], refs[2:-4], refs[-4:]
    else:
        received, (out, start) = refs[1:-2], refs[-2:]
    here = lax.axis_index("tm") == k
    steps = jac.shape[0]
    late = stage_bounds(steps)[3] if far else steps

    @pl.when(here)
    def _():
        for t in range(late, steps):
            jac_copy(jac_far, jac, sems, t).start()
        vector = received[0][...]
        for other in received[1:]:
            vector = vector + other[...]
        start[...] = vector
        keep = lax.axis_index("col") < 2 if k <= MERGE else None
        done = 1 + factors(k, steps)
        vector = apply_whole(whole, masked(keep, offset[...]), vector)
        if done < late:
            vector = run_steps(jac, inc, done, late, vector, keep)
        for t in range(late, steps):
            jac_copy(jac_far, jac, sems, t).wait()
            vector = step(jac, inc, t, vector, keep)
        out[...] = vector

    @pl.when(jnp.logical_not(here))
    def _():
        vector = kept[...]
        if joined:
            segment = lax.axis_index("tm")
            joins = functools.reduce(jnp.logical_or, [segment == other for other in joined])
            vector = jnp.where(joins, vector + received[0][...], vector)
        start[...] = vector
        out[...] = vector


def write_states(segment, jac, inc, rows, offs, vector, out):
    steps, part = out.shape
    prepared = jnp.logical_and(segment > 0, factors(segment, steps) == steps - 1)

    @pl.when(prepared)
    def _():
        for t in range(steps):
            own = apply_block(lambda left, t=t: rows[t, :, pl.ds(left, LANES)], vector)
            out[pl.ds(t, 1), :] = own + offs[pl.ds(t, 1), :]

    @pl.when(jnp.logical_not(prepared))
    def _():
        def body(t, v):
            v = step(jac, inc, t, v)
            out[pl.ds(t, 1), :] = own_part(v, part)
            return v

        lax.fori_loop(0, steps, body, vector)


def states_kernel(last, jac, inc, rows, offs, kept, out):
    segment = lax.axis_index("tm")

    @pl.when(segment != last)
    def _():
        write_states(segment, jac, inc, rows, offs, kept[...], out)


def last_kernel(last, jac, inc, rows, offs, received, before, out, scratch, sem):
    del before
    segment = lax.axis_index("tm")

    @pl.when(segment == last)
    def _():
        write_states(segment, jac, inc, rows, offs, received[...], scratch)
        copy = pltpu.make_async_copy(scratch, out, sem)
        copy.start()
        copy.wait()


def call(kernel, outs, *args, limit=4 << 20, far=(), far_out=False, scratch=(), aliases=None, work=0):
    return pl.pallas_call(
        kernel,
        out_shape=outs,
        in_specs=[FAR if place in far else VMEM for place in range(len(args))],
        out_specs=jax.tree.map(lambda _: FAR if far_out else VMEM, outs),
        scratch_shapes=scratch,
        input_output_aliases=aliases or {},
        cost_estimate=pl.CostEstimate(flops=work, bytes_accessed=work, transcendentals=0),
        compiler_params=pltpu.CompilerParams(vmem_limit_bytes=limit),
    )(*args)


def body(jacobians, increments, initial):
    segments, parts = lax.axis_size("tm"), lax.axis_size("col")
    steps, order, _ = jacobians.shape
    width = initial.shape[0]
    f32 = jnp.float32
    row = pltpu.VMEM((1, order), f32)
    far = [
        pltpu.with_memory_space_constraint(array, pltpu.HBM)
        for array in (jacobians, increments, initial[None, :])
    ]
    jac, inc, sent, whole, offset, rows, offs = call(
        first_kernel,
        (
            pltpu.VMEM(jacobians.shape, f32),
            pltpu.VMEM(increments.shape, f32),
            pltpu.VMEM((1, 2 * order), f32),
            pltpu.VMEM((order, order), f32),
            row,
            pltpu.VMEM((steps, width, order), f32),
            pltpu.VMEM((steps, width), f32),
        ),
        *far,
        far=(0, 1, 2),
        limit=16 << 20,
        scratch=[pltpu.VMEM((1, width), f32), pltpu.SemaphoreType.DMA((steps + 2,))],
    )
    near = [jac, inc, whole, offset, rows, offs]

    def more(window):
        if window > 1 and all(
            first_factors(segment, steps) + window >= steps - 1
            for segment in range(window + 1, segments)
        ):
            return near
        jac, inc, *rest = near
        made = [pltpu.VMEM(array.shape, f32) for array in (jac, *rest)]
        jac, *rest = call(
            functools.partial(factor_kernel, window),
            made,
            far[0],
            jac,
            inc,
            *rest,
            far=(0,),
            limit=16 << 20,
            scratch=[pltpu.SemaphoreType.DMA((steps,))],
            aliases={1: 0, 3: 1, 4: 2, 5: 3, 6: 4},
            work=1 << 28,
        )
        return [jac, inc, *rest]

    theirs = swap_parts(sent)
    near = more(0)
    out, kept = call(join_kernel, (row, row), sent, theirs)
    last = segments - 1
    for k in range(1, segments):
        joined = JOINS.get(k - 1, ())
        if k == MERGE + 1:
            received = [
                hop(out, MERGE, 2 * twist, VIAS[twist] % segments, joined)
                for twist in range(parts // 2)
            ]
        else:
            received = [hop(out, k - 1, joined=joined)]
        near = more(k)
        jac, inc, whole, offset, rows, offs = near
        if k < last:
            first = k == 1
            out, kept, *moved = call(
                functools.partial(hop_kernel, k, joined, first),
                [row, row] + [pltpu.VMEM(jac.shape, f32)] * first,
                inc,
                whole,
                offset,
                kept,
                jac,
                *[far[0]] * first,
                *received,
                far=(5,) if first else (),
                scratch=[pltpu.SemaphoreType.DMA((steps,))] * first,
                aliases={4: 2} if first else None,
            )
            if first:
                (jac,) = moved
                near = [jac, *near[1:]]
    shape = jax.ShapeDtypeStruct((steps, width), f32)
    before = call(
        functools.partial(states_kernel, last),
        shape,
        jac,
        inc,
        rows,
        offs,
        kept,
        work=steps * order * order * 4,
    )
    return call(
        functools.partial(last_kernel, last),
        shape,
        jac,
        inc,
        rows,
        offs,
        received[0],
        before,
        far=(5,),
        far_out=True,
        scratch=[pltpu.VMEM((steps, width), f32), pltpu.SemaphoreType.DMA],
        aliases={5: 0},
    )


def solution(mesh):
    return jax.shard_map(
        body,
        mesh=mesh,
        in_specs=(P("tm", None, None), P("tm", None), P("col")),
        out_specs=P("tm", "col"),
        check_vma=False,
    )
```

```python
import functools

import jax
import jax.numpy as jnp
from jax import lax
from jax.experimental import pallas as pl
from jax.experimental.pallas import tpu as pltpu
from jax.sharding import PartitionSpec as P

AXES = ("tm", "col")
LANES = 128
MERGES = {2: ((0, None), (2, 0)), 3: ((0, None), (1, -2))}
JOINS = {
    1: ((0,), ()),
    2: ((1,), ()),
    3: ((2,), (0, 1)),
    4: ((3,), (2,)),
}
AHEAD = (0, 1, 4, 6, 8, 7, 6)
STAGES = (6, 10)
VMEM = pl.BlockSpec(memory_space=pltpu.VMEM)
FAR = pl.BlockSpec(memory_space=pltpu.HBM)


def smaller(a, b):
    return min(a, b) if isinstance(a, int) and isinstance(b, int) else jnp.minimum(a, b)


def first_factors(segment, steps):
    wanted = AHEAD[-1]
    for place in range(len(AHEAD) - 1):
        if isinstance(segment, int):
            wanted = AHEAD[place] if segment == place else wanted
        else:
            wanted = jnp.where(segment == place, AHEAD[place], wanted)
    return smaller(wanted, steps - 1)


def factors(segment, steps):
    return smaller(first_factors(segment, steps) + segment - 1, steps - 1)


def swap_routes(size, moved):
    target = dict(moved)
    for device in range(size):
        partner = device ^ 1
        if device not in target and partner < size and partner not in target:
            target[device] = partner
            target[partner] = device
    return sorted(target.items())


def hop(block, segment, twist=0, via=None, joined=()):
    segments, parts = lax.axis_size("tm"), lax.axis_size("col")
    moved = {}
    for part in range(parts):
        here = segment * parts + part
        there = (segment + 1) * parts + (part ^ twist)
        moved[here] = there
        if via is None:
            moved[there] = here ^ 1 if segment + 2 == segments and parts % 2 == 0 else here
        else:
            middle = via * parts + (part ^ twist)
            moved[there] = middle
            moved[middle] = here
        for other in joined:
            moved[other * parts + part] = other * parts + (part ^ 2)
    return lax.ppermute(block, AXES, swap_routes(segments * parts, moved))


def reduce_rows(total):
    diagonal = lax.broadcasted_iota(jnp.int32, (LANES, LANES), 0) == lax.broadcasted_iota(
        jnp.int32, (LANES, LANES), 1
    )
    column = jnp.sum(total, axis=1, keepdims=True)
    return jnp.sum(jnp.where(diagonal, column, 0.0), axis=0, keepdims=True)


def apply_block(rows_of, vector):
    total = None
    for left in range(0, vector.shape[1], LANES):
        term = rows_of(left) * vector[:, left : left + LANES]
        total = term if total is None else total + term
    return reduce_rows(total)


def apply_map(block_of, offset, vector):
    pieces = [
        apply_block(functools.partial(block_of, top), vector)
        for top in range(0, vector.shape[1], LANES)
    ]
    return jnp.concatenate(pieces, axis=1) + offset


def apply_whole(whole, offset, vector):
    return apply_map(
        lambda top, left: whole[pl.ds(top, LANES), pl.ds(left, LANES)], offset, vector
    )


def masked(keep, added):
    return added if keep is None else jnp.where(keep, added, jnp.zeros_like(added))


def step(jac, inc, t, vector, keep=None):
    return apply_map(
        lambda top, left: jac[t, pl.ds(top, LANES), pl.ds(left, LANES)],
        masked(keep, inc[pl.ds(t, 1), :]),
        vector,
    )


def run_steps(jac, inc, first, last, vector, keep):
    return lax.fori_loop(first, last, lambda t, v: step(jac, inc, t, v, keep), vector)


def own_part(vector, part):
    index = lax.axis_index("col")
    own = vector[:, 0:part]
    for other in range(1, vector.shape[1] // part):
        own = jnp.where(index == other, vector[:, other * part : (other + 1) * part], own)
    return own


def halves(value):
    high = value.astype(jnp.bfloat16)
    return high, (value - high.astype(jnp.float32)).astype(jnp.bfloat16)


def product(left, right):
    left_high, left_low = halves(left)
    right_high, right_low = halves(right)

    def dot(a, b):
        return jnp.dot(a, b, preferred_element_type=jnp.float32)

    return dot(left_high, right_high) + (dot(left_high, right_low) + dot(left_low, right_high))


def jac_copy(jac_far, jac, sems, t):
    return pltpu.make_async_copy(jac_far.at[t], jac.at[t], sems.at[t])


def stage_bounds(steps):
    return [0] + [min(stage, steps) for stage in STAGES] + [steps]


def add_factor(t, jac, inc, whole, rows, offs, carry):
    width = offs.shape[1]
    own_rows = pl.ds(pl.multiple_of(lax.axis_index("col") * width, width), width)
    whole[...] = product(jac[t], whole[...])
    carry = step(jac, inc, t, carry)
    rows[t] = whole[own_rows, :]
    offs[pl.ds(t, 1), :] = own_part(carry, width)
    return carry


def factor_kernel(window, jac_far, jac_in, inc, whole_in, offset_in, rows_in, offs_in, *refs):
    jac, whole, offset, rows, offs, sems = refs
    del jac_in, whole_in, offset_in, rows_in, offs_in
    steps = jac.shape[0]
    segment = lax.axis_index("tm")
    t = first_factors(segment, steps) + window
    bounds = stage_bounds(steps)
    late = range(*bounds[1:3]) if window == 1 else ()

    @pl.when(segment == 1)
    def _():
        for place in late:
            jac_copy(jac_far, jac, sems, place).start()

    @pl.when(jnp.logical_and(segment > window, t < steps))
    def _():
        offset[...] = add_factor(t, jac, inc, whole, rows, offs, offset[...])

    @pl.when(segment == 1)
    def _():
        for place in late:
            jac_copy(jac_far, jac, sems, place).wait()


def first_kernel(jac_far, inc_far, own_far, jac, inc, out, kept, whole, offset, rows, offs, own, sems):
    steps, order, _ = jac.shape
    width = own.shape[1]
    segment = lax.axis_index("tm")
    index = lax.axis_index("col")
    soon = stage_bounds(steps)[1]
    now = jnp.where(segment == 1, soon, steps)

    def arrived(t):
        jac_copy(jac_far, jac, sems, t).wait()

    small = [
        pltpu.make_async_copy(own_far, own, sems.at[steps]),
        pltpu.make_async_copy(inc_far, inc, sems.at[steps + 1]),
    ]
    for copy in small:
        copy.start()
    for t in range(soon):
        jac_copy(jac_far, jac, sems, t).start()

    @pl.when(segment != 1)
    def _():
        for t in range(soon, steps):
            jac_copy(jac_far, jac, sems, t).start()

    for copy in small:
        copy.wait()

    @pl.when(segment == 0)
    def _():
        block = own[...]
        zero = jnp.zeros_like(block)
        vector = jnp.concatenate(
            [jnp.where(index == place, block, zero) for place in range(order // width)], axis=1
        )
        kept[...] = vector

        def body(t, current):
            arrived(t)
            return step(jac, inc, t, current, index == 0)

        out[...] = lax.fori_loop(0, steps, body, vector)

    @pl.when(segment > 0)
    def _():
        own_rows = pl.ds(pl.multiple_of(index * width, width), width)
        arrived(0)
        whole[...] = jac[0]
        rows[0] = jac[0, own_rows, :]
        first = inc[0:1, :]
        offs[0:1, :] = own_part(first, width)
        count = first_factors(segment, steps)

        def body(t, carry):
            arrived(t)
            return add_factor(t, jac, inc, whole, rows, offs, carry)

        offset[...] = lax.fori_loop(1, 1 + count, body, first)

        def finish(t, carry):
            arrived(t)
            return carry

        lax.fori_loop(1 + count, now, finish, 0)


def leading(k):
    added = sum(
        twist for segment, turns in MERGES.items() if segment < k for twist, _ in turns
    )
    missing = lax.axis_size("col") - 1 - added
    return (lax.axis_index("col") & missing) == 0 if missing else None


def hop_kernel(k, joined, far, inc, whole, offset, kept, *refs):
    jac = refs[0]
    if far:
        jac_far, received, (out, start, jac, sems) = refs[1], refs[2:-4], refs[-4:]
    else:
        received, (out, start) = refs[1:-2], refs[-2:]
    here = lax.axis_index("tm") == k
    steps = jac.shape[0]
    late = stage_bounds(steps)[2] if far else steps

    @pl.when(here)
    def _():
        for t in range(late, steps):
            jac_copy(jac_far, jac, sems, t).start()
        vector = received[0][...]
        for other in received[1:]:
            vector = vector + other[...]
        start[...] = vector
        keep = leading(k)
        done = 1 + factors(k, steps)
        vector = apply_whole(whole, masked(keep, offset[...]), vector)
        if done < late:
            vector = run_steps(jac, inc, done, late, vector, keep)
        for t in range(late, steps):
            jac_copy(jac_far, jac, sems, t).wait()
            vector = step(jac, inc, t, vector, keep)
        out[...] = vector

    @pl.when(jnp.logical_not(here))
    def _():
        vector = kept[...]
        if joined:
            segment = lax.axis_index("tm")
            joins = functools.reduce(jnp.logical_or, [segment == other for other in joined])
            vector = jnp.where(joins, vector + received[0][...], vector)
        start[...] = vector
        out[...] = vector


def write_states(segment, jac, inc, rows, offs, vector, out):
    steps, part = out.shape
    prepared = jnp.logical_and(segment > 0, factors(segment, steps) == steps - 1)

    @pl.when(prepared)
    def _():
        for t in range(steps):
            own = apply_block(lambda left, t=t: rows[t, :, pl.ds(left, LANES)], vector)
            out[pl.ds(t, 1), :] = own + offs[pl.ds(t, 1), :]

    @pl.when(jnp.logical_not(prepared))
    def _():
        def body(t, v):
            v = step(jac, inc, t, v)
            out[pl.ds(t, 1), :] = own_part(v, part)
            return v

        lax.fori_loop(0, steps, body, vector)


def states_kernel(last, jac, inc, rows, offs, kept, out):
    segment = lax.axis_index("tm")

    @pl.when(segment != last)
    def _():
        write_states(segment, jac, inc, rows, offs, kept[...], out)


def last_kernel(last, jac, inc, rows, offs, received, before, out, scratch, sem):
    del before
    segment = lax.axis_index("tm")

    @pl.when(segment == last)
    def _():
        write_states(segment, jac, inc, rows, offs, received[...], scratch)
        copy = pltpu.make_async_copy(scratch, out, sem)
        copy.start()
        copy.wait()


def call(kernel, outs, *args, limit=4 << 20, far=(), far_out=False, scratch=(), aliases=None, work=0):
    return pl.pallas_call(
        kernel,
        out_shape=outs,
        in_specs=[FAR if place in far else VMEM for place in range(len(args))],
        out_specs=jax.tree.map(lambda _: FAR if far_out else VMEM, outs),
        scratch_shapes=scratch,
        input_output_aliases=aliases or {},
        cost_estimate=pl.CostEstimate(flops=work, bytes_accessed=work, transcendentals=0),
        compiler_params=pltpu.CompilerParams(vmem_limit_bytes=limit),
    )(*args)


def body(jacobians, increments, initial):
    segments, parts = lax.axis_size("tm"), lax.axis_size("col")
    steps, order, _ = jacobians.shape
    width = initial.shape[0]
    f32 = jnp.float32
    row = pltpu.VMEM((1, order), f32)
    far = [
        pltpu.with_memory_space_constraint(array, pltpu.HBM)
        for array in (jacobians, increments, initial[None, :])
    ]
    jac, inc, out, kept, whole, offset, rows, offs = call(
        first_kernel,
        (
            pltpu.VMEM(jacobians.shape, f32),
            pltpu.VMEM(increments.shape, f32),
            row,
            row,
            pltpu.VMEM((order, order), f32),
            row,
            pltpu.VMEM((steps, width, order), f32),
            pltpu.VMEM((steps, width), f32),
        ),
        *far,
        far=(0, 1, 2),
        limit=16 << 20,
        scratch=[pltpu.VMEM((1, width), f32), pltpu.SemaphoreType.DMA((steps + 2,))],
    )
    near = [jac, inc, whole, offset, rows, offs]

    def more(window):
        if window > 1 and all(
            first_factors(segment, steps) + window >= steps
            for segment in range(window + 1, segments)
        ):
            return near
        jac, inc, *rest = near
        made = [pltpu.VMEM(array.shape, f32) for array in (jac, *rest)]
        jac, *rest = call(
            functools.partial(factor_kernel, window),
            made,
            far[0],
            jac,
            inc,
            *rest,
            far=(0,),
            limit=16 << 20,
            scratch=[pltpu.SemaphoreType.DMA((steps,))],
            aliases={1: 0, 3: 1, 4: 2, 5: 3, 6: 4},
            work=1 << 28,
        )
        return [jac, inc, *rest]

    last = segments - 1
    for k in range(1, segments):
        near_joins, far_joins = JOINS.get(k - 1, ((), ()))
        joined = near_joins + far_joins
        received = [
            hop(out, k - 1, twist, None if via is None else via % segments, far_joins)
            for twist, via in MERGES.get(k - 1, ((0, None),))
        ]
        near = more(k)
        jac, inc, whole, offset, rows, offs = near
        if k < last:
            first = k == 1
            out, kept, *moved = call(
                functools.partial(hop_kernel, k, joined, first),
                [row, row] + [pltpu.VMEM(jac.shape, f32)] * first,
                inc,
                whole,
                offset,
                kept,
                jac,
                *[far[0]] * first,
                *received,
                far=(5,) if first else (),
                scratch=[pltpu.SemaphoreType.DMA((steps,))] * first,
                aliases={4: 2} if first else None,
            )
            if first:
                (jac,) = moved
                near = [jac, *near[1:]]
    shape = jax.ShapeDtypeStruct((steps, width), f32)
    before = call(
        functools.partial(states_kernel, last),
        shape,
        jac,
        inc,
        rows,
        offs,
        kept,
        work=steps * order * order * 4,
    )
    return call(
        functools.partial(last_kernel, last),
        shape,
        jac,
        inc,
        rows,
        offs,
        received[0],
        before,
        far=(5,),
        far_out=True,
        scratch=[pltpu.VMEM((steps, width), f32), pltpu.SemaphoreType.DMA],
        aliases={5: 0},
    )


def solution(mesh):
    return jax.shard_map(
        body,
        mesh=mesh,
        in_specs=(P("tm", None, None), P("tm", None), P("col")),
        out_specs=P("tm", "col"),
        check_vma=False,
    )
```

```python
import functools

import jax
import jax.numpy as jnp
from jax import lax
from jax.experimental import pallas as pl
from jax.experimental.pallas import tpu as pltpu
from jax.sharding import PartitionSpec as P

AXES = ("tm", "col")
LANES = 128
MERGES = {2: ((0, None), (2, 0)), 3: ((0, None), (1, -2))}
JOINS = {
    1: ((0,), ()),
    2: ((1,), ()),
    3: ((2,), (0, 1)),
    4: ((3,), (2,)),
}
AHEAD = (0, 2, 4, 6, 8, 7, 6)
STAGES = (8, 10)
VMEM = pl.BlockSpec(memory_space=pltpu.VMEM)
FAR = pl.BlockSpec(memory_space=pltpu.HBM)


def smaller(a, b):
    return min(a, b) if isinstance(a, int) and isinstance(b, int) else jnp.minimum(a, b)


def first_factors(segment, steps):
    wanted = AHEAD[-1]
    for place in range(len(AHEAD) - 1):
        if isinstance(segment, int):
            wanted = AHEAD[place] if segment == place else wanted
        else:
            wanted = jnp.where(segment == place, AHEAD[place], wanted)
    return smaller(wanted, steps - 1)


def factors(segment, steps):
    return smaller(first_factors(segment, steps) + segment - 1, steps - 1)


def swap_routes(size, moved):
    target = dict(moved)
    for device in range(size):
        partner = device ^ 1
        if device not in target and partner < size and partner not in target:
            target[device] = partner
            target[partner] = device
    return sorted(target.items())


def hop(block, segment, twist=0, via=None, joined=()):
    segments, parts = lax.axis_size("tm"), lax.axis_size("col")
    moved = {}
    for part in range(parts):
        here = segment * parts + part
        there = (segment + 1) * parts + (part ^ twist)
        moved[here] = there
        if via is None:
            moved[there] = here ^ 1 if segment + 2 == segments and parts % 2 == 0 else here
        else:
            middle = via * parts + (part ^ twist)
            moved[there] = middle
            moved[middle] = here
        for other in joined:
            moved[other * parts + part] = other * parts + (part ^ 2)
    return lax.ppermute(block, AXES, swap_routes(segments * parts, moved))


def reduce_rows(total):
    diagonal = lax.broadcasted_iota(jnp.int32, (LANES, LANES), 0) == lax.broadcasted_iota(
        jnp.int32, (LANES, LANES), 1
    )
    column = jnp.sum(total, axis=1, keepdims=True)
    return jnp.sum(jnp.where(diagonal, column, 0.0), axis=0, keepdims=True)


def apply_block(rows_of, vector):
    total = None
    for left in range(0, vector.shape[1], LANES):
        term = rows_of(left) * vector[:, left : left + LANES]
        total = term if total is None else total + term
    return reduce_rows(total)


def apply_map(block_of, offset, vector):
    pieces = [
        apply_block(functools.partial(block_of, top), vector)
        for top in range(0, vector.shape[1], LANES)
    ]
    return jnp.concatenate(pieces, axis=1) + offset


def apply_whole(whole, offset, vector):
    return apply_map(
        lambda top, left: whole[pl.ds(top, LANES), pl.ds(left, LANES)], offset, vector
    )


def masked(keep, added):
    return added if keep is None else jnp.where(keep, added, jnp.zeros_like(added))


def step(jac, inc, t, vector, keep=None):
    return apply_map(
        lambda top, left: jac[t, pl.ds(top, LANES), pl.ds(left, LANES)],
        masked(keep, inc[pl.ds(t, 1), :]),
        vector,
    )


def run_steps(jac, inc, first, last, vector, keep):
    return lax.fori_loop(first, last, lambda t, v: step(jac, inc, t, v, keep), vector)


def own_part(vector, part):
    index = lax.axis_index("col")
    own = vector[:, 0:part]
    for other in range(1, vector.shape[1] // part):
        own = jnp.where(index == other, vector[:, other * part : (other + 1) * part], own)
    return own


def halves(value):
    high = value.astype(jnp.bfloat16)
    return high, (value - high.astype(jnp.float32)).astype(jnp.bfloat16)


def product(left, right):
    left_high, left_low = halves(left)
    right_high, right_low = halves(right)

    def dot(a, b):
        return jnp.dot(a, b, preferred_element_type=jnp.float32)

    return dot(left_high, right_high) + (dot(left_high, right_low) + dot(left_low, right_high))


def jac_copy(jac_far, jac, sems, t):
    return pltpu.make_async_copy(jac_far.at[t], jac.at[t], sems.at[t])


def stage_bounds(steps):
    return [0] + [min(stage, steps) for stage in STAGES] + [steps]


def add_factor(t, jac, inc, whole, rows, offs, carry):
    width = offs.shape[1]
    own_rows = pl.ds(pl.multiple_of(lax.axis_index("col") * width, width), width)
    whole[...] = product(jac[t], whole[...])
    carry = step(jac, inc, t, carry)
    rows[t] = whole[own_rows, :]
    offs[pl.ds(t, 1), :] = own_part(carry, width)
    return carry


def factor_kernel(window, jac_far, jac_in, inc, whole_in, offset_in, rows_in, offs_in, *refs):
    jac, whole, offset, rows, offs, sems = refs
    del jac_in, whole_in, offset_in, rows_in, offs_in
    steps = jac.shape[0]
    segment = lax.axis_index("tm")
    t = first_factors(segment, steps) + window
    bounds = stage_bounds(steps)
    late = range(*bounds[1:3]) if window == 1 else ()

    @pl.when(segment == 1)
    def _():
        for place in late:
            jac_copy(jac_far, jac, sems, place).start()

    @pl.when(jnp.logical_and(segment > window, t < steps))
    def _():
        offset[...] = add_factor(t, jac, inc, whole, rows, offs, offset[...])

    @pl.when(segment == 1)
    def _():
        for place in late:
            jac_copy(jac_far, jac, sems, place).wait()


def first_kernel(jac_far, inc_far, own_far, jac, inc, out, kept, whole, offset, rows, offs, own, sems):
    steps, order, _ = jac.shape
    width = own.shape[1]
    segment = lax.axis_index("tm")
    index = lax.axis_index("col")
    soon = stage_bounds(steps)[1]
    now = jnp.where(segment == 1, soon, steps)

    def arrived(t):
        jac_copy(jac_far, jac, sems, t).wait()

    small = [
        pltpu.make_async_copy(own_far, own, sems.at[steps]),
        pltpu.make_async_copy(inc_far, inc, sems.at[steps + 1]),
    ]
    for copy in small:
        copy.start()
    for t in range(soon):
        jac_copy(jac_far, jac, sems, t).start()

    @pl.when(segment != 1)
    def _():
        for t in range(soon, steps):
            jac_copy(jac_far, jac, sems, t).start()

    for copy in small:
        copy.wait()

    @pl.when(segment == 0)
    def _():
        block = own[...]
        zero = jnp.zeros_like(block)
        vector = jnp.concatenate(
            [jnp.where(index == place, block, zero) for place in range(order // width)], axis=1
        )
        kept[...] = vector

        def body(t, current):
            arrived(t)
            return step(jac, inc, t, current, index == 0)

        out[...] = lax.fori_loop(0, steps, body, vector)

    @pl.when(segment > 0)
    def _():
        own_rows = pl.ds(pl.multiple_of(index * width, width), width)
        arrived(0)
        whole[...] = jac[0]
        rows[0] = jac[0, own_rows, :]
        first = inc[0:1, :]
        offs[0:1, :] = own_part(first, width)
        count = first_factors(segment, steps)

        def body(t, carry):
            arrived(t)
            return add_factor(t, jac, inc, whole, rows, offs, carry)

        offset[...] = lax.fori_loop(1, 1 + count, body, first)

        def finish(t, carry):
            arrived(t)
            return carry

        lax.fori_loop(1 + count, now, finish, 0)


def leading(k):
    added = sum(
        twist for segment, turns in MERGES.items() if segment < k for twist, _ in turns
    )
    missing = lax.axis_size("col") - 1 - added
    return (lax.axis_index("col") & missing) == 0 if missing else None


def hop_kernel(k, joined, far, inc, whole, offset, kept, *refs):
    jac = refs[0]
    if far:
        jac_far, received, (out, start, jac, sems) = refs[1], refs[2:-4], refs[-4:]
    else:
        received, (out, start) = refs[1:-2], refs[-2:]
    here = lax.axis_index("tm") == k
    steps = jac.shape[0]
    late = stage_bounds(steps)[2] if far else steps

    @pl.when(here)
    def _():
        for t in range(late, steps):
            jac_copy(jac_far, jac, sems, t).start()
        vector = received[0][...]
        for other in received[1:]:
            vector = vector + other[...]
        start[...] = vector
        keep = leading(k)
        done = 1 + factors(k, steps)
        vector = apply_whole(whole, masked(keep, offset[...]), vector)
        if done < late:
            vector = run_steps(jac, inc, done, late, vector, keep)
        for t in range(late, steps):
            jac_copy(jac_far, jac, sems, t).wait()
            vector = step(jac, inc, t, vector, keep)
        out[...] = vector

    @pl.when(jnp.logical_not(here))
    def _():
        vector = kept[...]
        if joined:
            segment = lax.axis_index("tm")
            joins = functools.reduce(jnp.logical_or, [segment == other for other in joined])
            vector = jnp.where(joins, vector + received[0][...], vector)
        start[...] = vector
        out[...] = vector


def write_states(segment, jac, inc, rows, offs, vector, out):
    steps, part = out.shape
    prepared = jnp.logical_and(segment > 0, factors(segment, steps) == steps - 1)

    @pl.when(prepared)
    def _():
        for t in range(steps):
            own = apply_block(lambda left, t=t: rows[t, :, pl.ds(left, LANES)], vector)
            out[pl.ds(t, 1), :] = own + offs[pl.ds(t, 1), :]

    @pl.when(jnp.logical_not(prepared))
    def _():
        def body(t, v):
            v = step(jac, inc, t, v)
            out[pl.ds(t, 1), :] = own_part(v, part)
            return v

        lax.fori_loop(0, steps, body, vector)


def states_kernel(last, jac, inc, rows, offs, kept, out):
    segment = lax.axis_index("tm")

    @pl.when(segment != last)
    def _():
        write_states(segment, jac, inc, rows, offs, kept[...], out)


def last_kernel(last, jac, inc, rows, offs, received, before, out, scratch, sem):
    del before
    segment = lax.axis_index("tm")

    @pl.when(segment == last)
    def _():
        write_states(segment, jac, inc, rows, offs, received[...], scratch)
        copy = pltpu.make_async_copy(scratch, out, sem)
        copy.start()
        copy.wait()


def call(kernel, outs, *args, limit=4 << 20, far=(), far_out=False, scratch=(), aliases=None, work=0):
    return pl.pallas_call(
        kernel,
        out_shape=outs,
        in_specs=[FAR if place in far else VMEM for place in range(len(args))],
        out_specs=jax.tree.map(lambda _: FAR if far_out else VMEM, outs),
        scratch_shapes=scratch,
        input_output_aliases=aliases or {},
        cost_estimate=pl.CostEstimate(flops=work, bytes_accessed=work, transcendentals=0),
        compiler_params=pltpu.CompilerParams(vmem_limit_bytes=limit),
    )(*args)


def body(jacobians, increments, initial):
    segments, parts = lax.axis_size("tm"), lax.axis_size("col")
    steps, order, _ = jacobians.shape
    width = initial.shape[0]
    f32 = jnp.float32
    row = pltpu.VMEM((1, order), f32)
    far = [
        pltpu.with_memory_space_constraint(array, pltpu.HBM)
        for array in (jacobians, increments, initial[None, :])
    ]
    jac, inc, out, kept, whole, offset, rows, offs = call(
        first_kernel,
        (
            pltpu.VMEM(jacobians.shape, f32),
            pltpu.VMEM(increments.shape, f32),
            row,
            row,
            pltpu.VMEM((order, order), f32),
            row,
            pltpu.VMEM((steps, width, order), f32),
            pltpu.VMEM((steps, width), f32),
        ),
        *far,
        far=(0, 1, 2),
        limit=16 << 20,
        scratch=[pltpu.VMEM((1, width), f32), pltpu.SemaphoreType.DMA((steps + 2,))],
    )
    near = [jac, inc, whole, offset, rows, offs]

    def more(window):
        if window > 1 and all(
            first_factors(segment, steps) + window >= steps
            for segment in range(window + 1, segments)
        ):
            return near
        jac, inc, *rest = near
        made = [pltpu.VMEM(array.shape, f32) for array in (jac, *rest)]
        jac, *rest = call(
            functools.partial(factor_kernel, window),
            made,
            far[0],
            jac,
            inc,
            *rest,
            far=(0,),
            limit=16 << 20,
            scratch=[pltpu.SemaphoreType.DMA((steps,))],
            aliases={1: 0, 3: 1, 4: 2, 5: 3, 6: 4},
            work=1 << 28,
        )
        return [jac, inc, *rest]

    last = segments - 1
    for k in range(1, segments):
        near_joins, far_joins = JOINS.get(k - 1, ((), ()))
        joined = near_joins + far_joins
        received = [
            hop(out, k - 1, twist, None if via is None else via % segments, far_joins)
            for twist, via in MERGES.get(k - 1, ((0, None),))
        ]
        near = more(k)
        jac, inc, whole, offset, rows, offs = near
        if k < last:
            first = k == 1
            out, kept, *moved = call(
                functools.partial(hop_kernel, k, joined, first),
                [row, row] + [pltpu.VMEM(jac.shape, f32)] * first,
                inc,
                whole,
                offset,
                kept,
                jac,
                *[far[0]] * first,
                *received,
                far=(5,) if first else (),
                scratch=[pltpu.SemaphoreType.DMA((steps,))] * first,
                aliases={4: 2} if first else None,
            )
            if first:
                (jac,) = moved
                near = [jac, *near[1:]]
    shape = jax.ShapeDtypeStruct((steps, width), f32)
    before = call(
        functools.partial(states_kernel, last),
        shape,
        jac,
        inc,
        rows,
        offs,
        kept,
        work=steps * order * order * 4,
    )
    return call(
        functools.partial(last_kernel, last),
        shape,
        jac,
        inc,
        rows,
        offs,
        received[0],
        before,
        far=(5,),
        far_out=True,
        scratch=[pltpu.VMEM((steps, width), f32), pltpu.SemaphoreType.DMA],
        aliases={5: 0},
    )


def solution(mesh):
    return jax.shard_map(
        body,
        mesh=mesh,
        in_specs=(P("tm", None, None), P("tm", None), P("col")),
        out_specs=P("tm", "col"),
        check_vma=False,
    )
```
